32 devices in a mesh: dp: 8 (over z, x), tensor: 4 (over y, core).
Axes of the slice: x: 2, y: 2, z: 4, core: 2. Of those that a mesh axis runs over, the one named last changes fastest.
Arguments:
- context: bfloat16 [2, 8192, 3072], P(None, 'dp', 'tensor'), may hold values from -6 to 6
- out_grad: bfloat16 [2, 8192, 3072], P(None, ('dp', 'tensor')), may hold values from -0.1875 to 0.1875
- error_in: bfloat16 [2, 24576, 3072], P(None, 'dp', 'tensor'), may hold values from -6 to 6
- right_init: float32 [2, 64, 3072], P(None, None, 'tensor'), may hold values from -6 to 6
Outputs:
- summed_update: bfloat16 [2, 3072, 3072], P(None, 'dp', 'tensor')
- error_out: bfloat16 [2, 24576, 3072], P(None, 'dp', 'tensor')
The draws below stay inside these ranges and needn't reach their ends.
All inputs are finite; a program needn't handle non-finite values.
Results may differ from the reference program's by a relative error of at most 0.015.
Values may be sent and summed in bfloat16 or wider, within the bound.
A program may use at most 128 MiB of HBM per device.

```python
import jax
import jax.numpy as jnp
from jax import lax

D = 3072
RANK = 64
LAYERS = 2
TOK_DEV = 1024
TOKENS = 8192
REPL_ROWS = 24576
N_DP = 8


def block_levels(key, shape, pieces, least, high):
    loudness = 1.0
    for dim, blocks in pieces:
        heights = jax.random.uniform(jax.random.fold_in(jax.random.fold_in(key, 6), dim), (blocks,), jnp.float32, least / len(pieces), high / len(pieces))
        loudness = loudness * jnp.repeat(jnp.exp(heights), shape[dim] // blocks).reshape((-1,) + (1,) * (len(shape) - 1 - dim))
    return loudness


def scatter_about(rng, dims, deviation, bound, split=(), held_as=jnp.bfloat16):
    result = jax.random.normal(rng, dims, jnp.float32) * deviation
    if len(split) > 0:
        result = block_levels(rng, dims, split, -0.22, 0.18) * result
    return jnp.clip(result, min=-bound, max=bound).astype(held_as)


def setup_inputs(seed: int = 0) -> dict:
    keys = jax.random.split(jax.random.key(seed), 5)
    context = scatter_about(keys[0], (LAYERS, TOKENS, D), 1.0, 6.0, ((1, 8), (2, 4)))
    out_grad = scatter_about(keys[1], (LAYERS, TOKENS, D), TOK_DEV ** -0.5, 0.1875, ((1, 32),))
    error_in = scatter_about(keys[2], (LAYERS, REPL_ROWS, D), 1.0, 6.0, ((1, 8), (2, 4)))
    right_init = scatter_about(keys[3], (LAYERS, RANK, D), 1.0, 6.0, ((2, 4),), jnp.float32)
    return {"context": context, "out_grad": out_grad, "error_in": error_in, "right_init": right_init}


def ortho_rows(left_factor):
    gram_matrix = jnp.dot(left_factor, left_factor.T, precision=lax.Precision.HIGHEST)
    ridge_term = 1e-06 * jnp.mean(jnp.diagonal(gram_matrix))
    gram_matrix = gram_matrix + ridge_term * jnp.eye(gram_matrix.shape[0], dtype=gram_matrix.dtype)
    factor_low = jnp.linalg.cholesky(gram_matrix)
    return jax.scipy.linalg.solve_triangular(factor_low, left_factor, lower=True)

def reference(context, out_grad, error_in, right_init):
    summed_list = []
    error_list = []
    for layer in range(LAYERS):
        ctx_blocks = context[layer].reshape(N_DP, TOK_DEV, D)
        grad_blocks = out_grad[layer].reshape(N_DP, TOK_DEV, D)
        err_blocks = error_in[layer].reshape(N_DP, D, D)

        def one_moment(items):
            return jnp.dot(items[1].T.astype(jnp.float32), items[0].astype(jnp.float32), preferred_element_type=jnp.float32) + items[2].astype(jnp.float32)
        moments = lax.map(one_moment, (ctx_blocks, grad_blocks, err_blocks))
        left_factor = jnp.einsum('re,nde->rd', right_init[layer], moments, precision=lax.Precision.HIGHEST)
        ortho_basis = ortho_rows(left_factor)
        right_factor = jnp.einsum('rd,nde->re', ortho_basis, moments, precision=lax.Precision.HIGHEST)
        summed = jnp.dot(ortho_basis.T, right_factor, precision=lax.Precision.HIGHEST)
        summed_list.append(summed.astype(jnp.bfloat16))
        mean_part = jnp.dot(ortho_basis.T, right_factor / N_DP, precision=lax.Precision.HIGHEST)
        new_error = (moments - mean_part[None]).astype(jnp.bfloat16)
        error_list.append(new_error.reshape(N_DP * D, D))
    return (jnp.stack(summed_list), jnp.stack(error_list))
```

```python
import functools

import jax
import jax.numpy as jnp
from jax import lax
from jax.experimental import pallas as pl
from jax.experimental.pallas import tpu as pltpu
from jax.sharding import PartitionSpec as P

MESH = pl.DeviceIdType.MESH
HIGHEST = lax.Precision.HIGHEST
F32 = jnp.float32
BF16 = jnp.bfloat16
LEFT_WIRE = jnp.float32
CHUNKS = 8


def split(value):
    high = value.astype(BF16)
    return high, (value - high.astype(F32)).astype(BF16)


def dot(a, b, dims):
    return lax.dot_general(a, b, (dims, ((), ())), preferred_element_type=F32)


def inverse_factors(grams):
    size = grams[0].shape[0]
    rows = lax.broadcasted_iota(jnp.int32, (size, size), 0)
    cols = lax.broadcasted_iota(jnp.int32, (size, size), 1)
    eye = (rows == cols).astype(F32)
    wide_rows = lax.broadcasted_iota(jnp.int32, (size, 2 * size), 0)
    work = []
    for gram in grams:
        mean = jnp.sum(jnp.sum(gram * eye, axis=1, keepdims=True), axis=0, keepdims=True) / size
        work.append(jnp.concatenate([gram + (1e-06 * mean) * eye, eye], axis=1))
    scales = [jnp.zeros((size, 1), F32) for _ in grams]
    one_col = wide_rows[:, :1]
    for k in range(size):
        for i, full in enumerate(work):
            row = full[k : k + 1, :]
            pivot = full[k : k + 1, k : k + 1]
            ratio = jnp.where(one_col > k, full[:, k : k + 1] / pivot, 0.0)
            scales[i] = jnp.where(one_col == k, lax.rsqrt(pivot), scales[i])
            work[i] = full - ratio * row
    return [full[:, size:] * scale for full, scale in zip(work, scales)]


def comm_kernel(
    n_d,
    n_t,
    x_hbm,
    y_hbm,
    e_hbm,
    r_hbm,
    yfull,
    ot_ref,
    right_ref,
    x_ref,
    y_ref,
    e_ref,
    r_ref,
    pt,
    pt_in,
    q_all,
    lt,
    lt_core,
    lt_send,
    lt_in,
    lt_y,
    lt_sum,
    ltf,
    r_send,
    r_in,
    r_all,
    local_sems,
    yl_sem,
    y_send,
    y_recv,
    f_send,
    f_recv,
    p_send,
    p_recv,
    c_send,
    c_recv,
    d_send,
    d_recv,
    s_send,
    s_recv,
    g_send,
    g_recv,
    h_send,
    h_recv,
    q_send,
    q_recv,
    a_send,
    a_recv,
    b_send,
    b_recv,
):
    layers, own, width = y_ref.shape
    feats = x_ref.shape[2]
    rank = r_ref.shape[1]
    d = lax.axis_index("dp")
    t = lax.axis_index("tensor")
    core = lax.rem(t, 2)
    partner = t + 1 - 2 * core
    n_y = n_t // 2
    half = width // 2
    piece = half // n_d

    def remote(src, dst, send, recv, where):
        return pltpu.make_async_remote_copy(
            src_ref=src, dst_ref=dst, send_sem=send, recv_sem=recv, device_id=where, device_id_type=MESH
        )

    loads = [
        pltpu.make_async_copy(a, b, local_sems.at[i])
        for i, (a, b) in enumerate(((r_hbm, r_ref), (x_hbm, x_ref), (y_hbm, y_ref), (e_hbm, e_ref)))
    ]
    for load in loads:
        load.start()

    barrier = pltpu.get_barrier_semaphore()
    for k in range(1, n_d):
        pl.semaphore_signal(barrier, inc=1, device_id={"dp": lax.rem(d + k, n_d)}, device_id_type=MESH)
    for k in range(1, n_t):
        pl.semaphore_signal(barrier, inc=1, device_id={"tensor": lax.rem(t + k, n_t)}, device_id_type=MESH)
    pl.semaphore_wait(barrier, n_d + n_t - 2)

    rows = own // CHUNKS
    my_rows = pl.ds(pl.multiple_of(t * own, own), own)
    chunks = [(layer, c) for layer in range(layers) for c in range(CHUNKS)]

    def chunk_copy(i, m):
        layer, c = chunks[i]
        there = lax.rem(t + 2 * m, n_t)
        return remote(
            y_hbm.at[layer, pl.ds(c * rows, rows), :],
            yfull.at[layer, pl.ds(pl.multiple_of(t * own + c * rows, rows), rows), :],
            y_send.at[m - 1, i],
            y_recv.at[m - 1, i],
            {"tensor": there},
        )

    def chunk_in(i, m):
        layer, c = chunks[i]
        source = lax.rem(t + n_t - 2 * m, n_t)
        here = yfull.at[layer, pl.ds(pl.multiple_of(source * own + c * rows, rows), rows), :]
        return here, remote(
            y_hbm.at[layer, pl.ds(c * rows, rows), :], here, y_send.at[m - 1, i], y_recv.at[m - 1, i], {"tensor": source}
        )

    def forward_copy(i, m):
        here, _ = chunk_in(i, m)
        return remote(here, here, f_send.at[m, i], f_recv.at[m, i], {"tensor": partner})

    def forward_in(i, m):
        layer, c = chunks[i]
        source = lax.rem(partner + n_t - 2 * m, n_t)
        here = yfull.at[layer, pl.ds(pl.multiple_of(source * own + c * rows, rows), rows), :]
        return remote(here, here, f_send.at[m, i], f_recv.at[m, i], {"tensor": partner})

    sent = [0]
    passed = [0]

    def send_chunks(count):
        for i in range(sent[0], min(sent[0] + count, len(chunks))):
            for m in range(1, n_y):
                chunk_copy(i, m).start()
        sent[0] = min(sent[0] + count, len(chunks))

    def pass_chunks(upto):
        for i in range(passed[0], min(upto, len(chunks))):
            for m in range(1, n_y):
                chunk_in(i, m)[1].wait_recv()
                forward_copy(i, m).start()
        passed[0] = max(passed[0], min(upto, len(chunks)))

    send_chunks(2)
    own_copy = remote(y_hbm, yfull.at[:, my_rows, :], f_send.at[0, 0], f_recv.at[0, 0], {"tensor": partner})
    own_copy.start()
    partner_rows = pl.ds(pl.multiple_of(partner * own, own), own)
    own_in = remote(y_hbm, yfull.at[:, partner_rows, :], f_send.at[0, 0], f_recv.at[0, 0], {"tensor": partner})

    loads[0].wait()
    loads[1].wait()
    r_parts = [split(r_ref[layer]) for layer in range(layers)]
    tiles = x_ref.shape[1] // own
    for tile in range(tiles):
        outs = []
        for layer in range(layers):
            block = x_ref[layer, tile * own : (tile + 1) * own, :]
            high, low = r_parts[layer]
            outs.append(dot(block, high, ((1,), (1,))) + dot(block, low, ((1,), (1,))))
        pt[tile] = jnp.concatenate(outs, axis=1)

    p_out = []
    for k in range(1, n_t):
        there = lax.rem(t + k, n_t)
        copy = remote(pt.at[there], pt_in.at[k - 1], p_send.at[k - 1], p_recv.at[k - 1], {"tensor": there})
        copy.start()
        p_out.append(copy)
    send_chunks(3)

    loads[3].wait()
    loads[2].wait()
    own_y = pltpu.make_async_copy(y_ref, yfull.at[:, my_rows, :], yl_sem)
    own_y.start()
    block_rows = width // 6

    def left_of_error(i, carry):
        at = pl.ds(pl.multiple_of(i * block_rows, block_rows), block_rows)
        outs = []
        for layer in range(layers):
            block = e_ref[layer, at, :]
            high, low = r_parts[layer]
            outs.append(dot(block, high, ((1,), (1,))) + dot(block, low, ((1,), (1,))))
        lt[at, :] = jnp.concatenate(outs, axis=1)
        return carry

    lax.fori_loop(0, 6, left_of_error, 0)
    for copy in p_out:
        copy.wait()
    total = pt[t]
    for k in range(n_t - 1):
        total = total + pt_in[k]
    p_parts = [split(total[:, layer * rank : (layer + 1) * rank]) for layer in range(layers)]

    def left_of_tokens(i, carry):
        at = pl.ds(pl.multiple_of(i * block_rows, block_rows), block_rows)
        outs = []
        for layer in range(layers):
            block = y_ref[layer, :, at]
            high, low = p_parts[layer]
            outs.append(dot(block, high, ((0,), (0,))) + dot(block, low, ((0,), (0,))))
        lt[at, :] += jnp.concatenate(outs, axis=1)
        return carry

    lax.fori_loop(0, 6, left_of_tokens, 0)

    mine = pl.multiple_of(core * half, half)
    other = pl.multiple_of((1 - core) * half, half)
    core_copy = remote(lt.at[pl.ds(other, half), :], lt_core, c_send, c_recv, {"tensor": partner})
    core_copy.start()
    core_copy.wait()

    def add_core(j, carry):
        at = pl.ds(pl.multiple_of(mine + j * piece, piece), piece)
        value = lt[at, :] + lt_core[pl.ds(pl.multiple_of(j * piece, piece), piece), :]
        lt_send[j] = value.astype(lt_send.dtype)
        return carry

    lax.fori_loop(0, n_d, add_core, 0)
    d_out = []
    for k in range(1, n_d):
        there = lax.rem(d + k, n_d)
        copy = remote(lt_send.at[there], lt_in.at[k - 1], d_send.at[k - 1], d_recv.at[k - 1], {"dp": there})
        copy.start()
        d_out.append(copy)
    send_chunks(4)
    pass_chunks(2)
    for copy in d_out:
        copy.wait()
    total = lt_send[d].astype(F32)
    for k in range(n_d - 1):
        total = total + lt_in[k].astype(F32)
    lt_sum[...] = total
    s_out = []
    for m in range(1, n_y):
        there = lax.rem(t + 2 * m, n_t)
        copy = remote(lt_sum, lt_y.at[m - 1], s_send.at[m - 1], s_recv.at[m - 1], {"tensor": there})
        copy.start()
        s_out.append(copy)
    send_chunks(3)
    for copy in s_out:
        copy.wait()
    for m in range(n_y - 1):
        total = total + lt_y[m]

    def slot(side, index):
        return ltf.at[pl.ds(pl.multiple_of(side * half + index * piece, piece), piece), :]

    ltf[pl.ds(pl.multiple_of(mine + d * piece, piece), piece), :] = total.astype(ltf.dtype)
    g_out = []
    for k in range(1, n_d):
        there = lax.rem(d + k, n_d)
        copy = remote(slot(core, d), slot(core, d), g_send.at[k - 1], g_recv.at[k - 1], {"dp": there})
        copy.start()
        g_out.append(copy)
    h_out = []
    for k in range(n_d):
        source = lax.rem(d + n_d - k, n_d)
        if k > 0:
            remote(slot(core, source), slot(core, source), g_send.at[k - 1], g_recv.at[k - 1], {"dp": source}).wait_recv()
        copy = remote(slot(core, source), slot(core, source), h_send.at[k], h_recv.at[k], {"tensor": partner})
        copy.start()
        h_out.append(copy)
    send_chunks(3)
    pass_chunks(7)
    for k in range(n_d):
        source = lax.rem(d + n_d - k, n_d)
        remote(
            slot(1 - core, source), slot(1 - core, source), h_send.at[k], h_recv.at[k], {"tensor": partner}
        ).wait_recv()
    for copy in g_out + h_out:
        copy.wait_send()

    gram = jnp.zeros((layers * rank, layers * rank), F32)
    for i in range(6):
        block = ltf[i * block_rows : (i + 1) * block_rows, :].astype(F32)
        gram = gram + lax.dot_general(
            block, block, (((0,), (0,)), ((), ())), precision=HIGHEST, preferred_element_type=F32
        )
    grams = [gram[k * rank : (k + 1) * rank, k * rank : (k + 1) * rank] for k in range(layers)]
    inverses = inverse_factors(grams)
    zero = jnp.zeros((rank, rank), F32)
    spread = jnp.concatenate(
        [
            jnp.concatenate([inverses[i] if i == j else zero for j in range(layers)], axis=1)
            for i in range(layers)
        ],
        axis=0,
    )

    q = [jnp.zeros((own, 2 * rank), F32) for _ in range(layers)]
    right = [jnp.zeros((2 * rank, feats), F32) for _ in range(layers)]
    for i in range(6):
        at = slice(i * block_rows, (i + 1) * block_rows)
        basis = lax.dot_general(
            ltf[at, :].astype(F32), spread, (((1,), (1,)), ((), ())), precision=HIGHEST, preferred_element_type=F32
        )
        ot_ref[at, :] = basis
        for layer in range(layers):
            both = jnp.concatenate(split(basis[:, layer * rank : (layer + 1) * rank]), axis=1)
            q[layer] = q[layer] + dot(y_ref[layer, :, at], both, ((1,), (0,)))
    q_all[t] = jnp.concatenate([part[:, :rank] + part[:, rank:] for part in q], axis=1)
    q_out = []
    for k in range(1, n_t):
        copy = remote(
            q_all.at[t], q_all.at[t], q_send.at[k - 1], q_recv.at[k - 1], {"tensor": lax.rem(t + k, n_t)}
        )
        copy.start()
        q_out.append(copy)
    send_chunks(len(chunks))
    for i in range(6):
        at = slice(i * block_rows, (i + 1) * block_rows)
        for layer in range(layers):
            both = jnp.concatenate(split(ot_ref[at, layer * rank : (layer + 1) * rank]), axis=1)
            right[layer] = right[layer] + dot(both, e_ref[layer, at, :], ((0,), (0,)))
    for k in range(1, n_t):
        source = lax.rem(t + n_t - k, n_t)
        remote(
            q_all.at[source], q_all.at[source], q_send.at[k - 1], q_recv.at[k - 1], {"tensor": source}
        ).wait_recv()
    for tile in range(tiles):
        value = q_all[tile]
        for layer in range(layers):
            both = jnp.concatenate(split(value[:, layer * rank : (layer + 1) * rank]), axis=1)
            right[layer] = right[layer] + dot(both, x_ref[layer, tile * own : (tile + 1) * own, :], ((0,), (0,)))
    right_rows = jnp.concatenate([part[:rank] + part[rank:] for part in right], axis=0)
    share = layers * rank // n_d
    for j in range(n_d):
        r_send[j] = right_rows[j * share : (j + 1) * share, :].astype(BF16)
    a_out = []
    for k in range(1, n_d):
        there = lax.rem(d + k, n_d)
        copy = remote(r_send.at[there], r_in.at[k - 1], a_send.at[k - 1], a_recv.at[k - 1], {"dp": there})
        copy.start()
        a_out.append(copy)
    pass_chunks(10)
    for copy in a_out:
        copy.wait()
    total = r_send[d].astype(F32)
    for k in range(n_d - 1):
        total = total + r_in[k].astype(F32)
    r_all[d] = total.astype(BF16)
    b_out = []
    for k in range(1, n_d):
        copy = remote(r_all.at[d], r_all.at[d], b_send.at[k - 1], b_recv.at[k - 1], {"dp": lax.rem(d + k, n_d)})
        copy.start()
        b_out.append(copy)
    pass_chunks(len(chunks))
    for k in range(1, n_d):
        source = lax.rem(d + n_d - k, n_d)
        remote(r_all.at[source], r_all.at[source], b_send.at[k - 1], b_recv.at[k - 1], {"dp": source}).wait_recv()
    right_ref[...] = r_all[...]
    own_in.wait_recv()
    own_copy.wait_send()
    own_y.wait()
    for copy in q_out + b_out:
        copy.wait_send()
    for i in range(len(chunks)):
        for m in range(1, n_y):
            chunk_copy(i, m).wait_send()
            forward_copy(i, m).wait_send()
            forward_in(i, m).wait_recv()


def error_kernel(n_d, y_ref, x_ref, e_ref, o_ref, r_ref, own_ref, err_ref, sum_ref):
    layer = pl.program_id(0)
    rank = r_ref.shape[1]

    def low_rank(basis):
        high, low = split(basis)
        return dot(high, r_ref[0], ((1,), (0,))) + dot(low, r_ref[0], ((1,), (0,)))

    moment = dot(y_ref[0], x_ref[0], ((0,), (0,))) + e_ref[0].astype(F32)
    err_ref[0] = (moment - low_rank(o_ref[0]) * (1.0 / n_d)).astype(err_ref.dtype)

    @pl.when(pl.program_id(1) == 0)
    def _():
        sum_ref[0] = low_rank(own_ref[0]).astype(sum_ref.dtype)


def solution(mesh):
    n_d, n_t = mesh.shape["dp"], mesh.shape["tensor"]

    def body(context, out_grad, error_in, right_init):
        layers, tokens, feats = context.shape
        own, width = out_grad.shape[1:]
        rank = right_init.shape[1]
        wide = layers * rank
        half = width // 2
        piece = half // n_d
        share = wide // n_d
        n_y = n_t // 2
        n_c = layers * CHUNKS
        dma = pltpu.SemaphoreType.DMA
        any_spec = pl.BlockSpec(memory_space=pl.ANY)
        vmem_spec = pl.BlockSpec(memory_space=pltpu.VMEM)
        pairs = lambda *shape: [dma(shape), dma(shape)]
        yfull, ortho, right = pl.pallas_call(
            functools.partial(comm_kernel, n_d, n_t),
            name="low_rank_chain",
            out_shape=(
                jax.ShapeDtypeStruct((layers, tokens, width), BF16),
                jax.ShapeDtypeStruct((width, wide), F32),
                jax.ShapeDtypeStruct((n_d, share, feats), BF16),
            ),
            in_specs=[any_spec] * 4,
            out_specs=(any_spec, vmem_spec, vmem_spec),
            scratch_shapes=[
                pltpu.VMEM((layers, tokens, feats), BF16),
                pltpu.VMEM((layers, own, width), BF16),
                pltpu.VMEM((layers, width, feats), BF16),
                pltpu.VMEM((layers, rank, feats), F32),
                pltpu.VMEM((n_t, own, wide), F32),
                pltpu.VMEM((n_t - 1, own, wide), F32),
                pltpu.VMEM((n_t, own, wide), F32),
                pltpu.VMEM((width, wide), F32),
                pltpu.VMEM((half, wide), F32),
                pltpu.VMEM((n_d, piece, wide), LEFT_WIRE),
                pltpu.VMEM((n_d - 1, piece, wide), LEFT_WIRE),
                pltpu.VMEM((max(n_y - 1, 1), piece, wide), F32),
                pltpu.VMEM((piece, wide), F32),
                pltpu.VMEM((width, wide), LEFT_WIRE),
                pltpu.VMEM((n_d, share, feats), BF16),
                pltpu.VMEM((n_d - 1, share, feats), BF16),
                pltpu.VMEM((n_d, share, feats), BF16),
                dma((4,)),
                dma,
            ]
            + pairs(max(n_y - 1, 1), n_c)
            + pairs(n_y, n_c)
            + pairs(n_t - 1)
            + [dma, dma]
            + pairs(n_d - 1)
            + pairs(max(n_y - 1, 1))
            + pairs(n_d - 1)
            + pairs(n_d)
            + pairs(n_t - 1)
            + pairs(n_d - 1)
            + pairs(n_d - 1),
            compiler_params=pltpu.CompilerParams(
                collective_id=0, has_side_effects=True, vmem_limit_bytes=60 * 1024 * 1024
            ),
        )(context, out_grad, error_in, right_init)
        ortho = jnp.transpose(ortho.reshape(width, layers, rank), (1, 0, 2))
        right = right.reshape(layers, rank, feats)
        rows = width // n_d
        own_basis = lax.dynamic_slice_in_dim(ortho, lax.axis_index("dp") * rows, rows, 1)
        tile = width // 6
        new_error, summed = pl.pallas_call(
            functools.partial(error_kernel, n_d),
            name="new_error",
            grid=(layers, width // tile),
            out_shape=(
                jax.ShapeDtypeStruct((layers, width, feats), BF16),
                jax.ShapeDtypeStruct((layers, rows, feats), BF16),
            ),
            in_specs=[
                pl.BlockSpec((1, tokens, tile), lambda i, j: (i, 0, j)),
                pl.BlockSpec((1, tokens, feats), lambda i, j: (i, 0, 0)),
                pl.BlockSpec((1, tile, feats), lambda i, j: (i, j, 0)),
                pl.BlockSpec((1, tile, rank), lambda i, j: (i, j, 0)),
                pl.BlockSpec((1, rank, feats), lambda i, j: (i, 0, 0)),
                pl.BlockSpec((1, rows, rank), lambda i, j: (i, 0, 0)),
            ],
            out_specs=(
                pl.BlockSpec((1, tile, feats), lambda i, j: (i, j, 0)),
                pl.BlockSpec((1, rows, feats), lambda i, j: (i, 0, 0)),
            ),
            compiler_params=pltpu.CompilerParams(
                dimension_semantics=("arbitrary", "arbitrary"), vmem_limit_bytes=48 * 1024 * 1024
            ),
        )(yfull, context, error_in, ortho, right, own_basis)
        return summed, new_error

    return jax.shard_map(
        body,
        mesh=mesh,
        in_specs=(
            P(None, "dp", "tensor"),
            P(None, ("dp", "tensor"), None),
            P(None, "dp", "tensor"),
            P(None, None, "tensor"),
        ),
        out_specs=(P(None, "dp", "tensor"), P(None, "dp", "tensor")),
        check_vma=False,
    )
```

```python
import functools

import jax
import jax.numpy as jnp
from jax import lax
from jax.experimental import pallas as pl
from jax.experimental.pallas import tpu as pltpu
from jax.sharding import PartitionSpec as P

MESH = pl.DeviceIdType.MESH
HIGHEST = lax.Precision.HIGHEST
F32 = jnp.float32
BF16 = jnp.bfloat16
WIRE = jnp.bfloat16
CHUNKS = 8
PLAN = (2, 3, 1, 6, 0, 16)


def split(value):
    high = value.astype(BF16)
    return high, (value - high.astype(F32)).astype(BF16)


def dot(a, b, dims):
    return lax.dot_general(a, b, (dims, ((), ())), preferred_element_type=F32)


def inverse_factors(grams):
    size = grams[0].shape[0]
    rows = lax.broadcasted_iota(jnp.int32, (size, size), 0)
    cols = lax.broadcasted_iota(jnp.int32, (size, size), 1)
    eye = (rows == cols).astype(F32)
    wide_rows = lax.broadcasted_iota(jnp.int32, (size, 2 * size), 0)
    work = []
    for gram in grams:
        mean = jnp.sum(jnp.sum(gram * eye, axis=1, keepdims=True), axis=0, keepdims=True) / size
        work.append(jnp.concatenate([gram + (1e-06 * mean) * eye, eye], axis=1))
    scales = [jnp.zeros((size, 1), F32) for _ in grams]
    one_col = wide_rows[:, :1]
    for k in range(size):
        for i, full in enumerate(work):
            row = full[k : k + 1, :]
            pivot = full[k : k + 1, k : k + 1]
            ratio = jnp.where(one_col > k, full[:, k : k + 1] / pivot, 0.0)
            scales[i] = jnp.where(one_col == k, lax.rsqrt(pivot), scales[i])
            work[i] = full - ratio * row
    return [full[:, size:] * scale for full, scale in zip(work, scales)]


def comm_kernel(
    n_d,
    n_t,
    x_hbm,
    y_hbm,
    e_hbm,
    r_hbm,
    yfull,
    ot_ref,
    own_ref,
    right_ref,
    x_ref,
    y_ref,
    e_ref,
    r_ref,
    pt,
    pt_in,
    q_all,
    lt,
    lt_core,
    lt_send,
    lt_in,
    lt_y,
    lt_sum,
    ltf,
    r_send,
    r_in,
    r_all,
    local_sems,
    yl_sem,
    y_send,
    y_recv,
    f_send,
    f_recv,
    p_send,
    p_recv,
    c_send,
    c_recv,
    d_send,
    d_recv,
    s_send,
    s_recv,
    g_send,
    g_recv,
    h_send,
    h_recv,
    q_send,
    q_recv,
    a_send,
    a_recv,
    b_send,
    b_recv,
):
    layers, own, width = y_ref.shape
    feats = x_ref.shape[2]
    rank = r_ref.shape[1]
    d = lax.axis_index("dp")
    t = lax.axis_index("tensor")
    core = lax.rem(t, 2)
    partner = t + 1 - 2 * core
    n_y = n_t // 2
    half = width // 2
    piece = half // n_d

    def remote(src, dst, send, recv, where):
        return pltpu.make_async_remote_copy(
            src_ref=src, dst_ref=dst, send_sem=send, recv_sem=recv, device_id=where, device_id_type=MESH
        )

    loads = [
        pltpu.make_async_copy(a, b, local_sems.at[i])
        for i, (a, b) in enumerate(((r_hbm, r_ref), (x_hbm, x_ref), (y_hbm, y_ref), (e_hbm, e_ref)))
    ]
    for load in loads:
        load.start()

    barrier = pltpu.get_barrier_semaphore()
    for k in range(1, n_d):
        pl.semaphore_signal(barrier, inc=1, device_id={"dp": lax.rem(d + k, n_d)}, device_id_type=MESH)
    for k in range(1, n_t):
        pl.semaphore_signal(barrier, inc=1, device_id={"tensor": lax.rem(t + k, n_t)}, device_id_type=MESH)
    pl.semaphore_wait(barrier, n_d + n_t - 2)

    rows = own // CHUNKS
    my_rows = pl.ds(pl.multiple_of(t * own, own), own)
    chunks = [(layer, c) for layer in range(layers) for c in range(CHUNKS)]

    def chunk_copy(i, m):
        layer, c = chunks[i]
        there = lax.rem(t + 2 * m, n_t)
        return remote(
            y_hbm.at[layer, pl.ds(c * rows, rows), :],
            yfull.at[layer, pl.ds(pl.multiple_of(t * own + c * rows, rows), rows), :],
            y_send.at[m - 1, i],
            y_recv.at[m - 1, i],
            {"tensor": there},
        )

    def chunk_in(i, m):
        layer, c = chunks[i]
        source = lax.rem(t + n_t - 2 * m, n_t)
        here = yfull.at[layer, pl.ds(pl.multiple_of(source * own + c * rows, rows), rows), :]
        return here, remote(
            y_hbm.at[layer, pl.ds(c * rows, rows), :], here, y_send.at[m - 1, i], y_recv.at[m - 1, i], {"tensor": source}
        )

    def forward_copy(i, m):
        here, _ = chunk_in(i, m)
        return remote(here, here, f_send.at[m, i], f_recv.at[m, i], {"tensor": partner})

    def forward_in(i, m):
        layer, c = chunks[i]
        source = lax.rem(partner + n_t - 2 * m, n_t)
        here = yfull.at[layer, pl.ds(pl.multiple_of(source * own + c * rows, rows), rows), :]
        return remote(here, here, f_send.at[m, i], f_recv.at[m, i], {"tensor": partner})

    sent = [0]
    passed = [0]

    def send_chunks(count):
        for i in range(sent[0], min(sent[0] + count, len(chunks))):
            for m in range(1, n_y):
                chunk_copy(i, m).start()
        sent[0] = min(sent[0] + count, len(chunks))

    def pass_chunks(upto):
        for i in range(passed[0], min(upto, len(chunks))):
            for m in range(1, n_y):
                chunk_in(i, m)[1].wait_recv()
                forward_copy(i, m).start()
        passed[0] = max(passed[0], min(upto, len(chunks)))

    send_chunks(PLAN[0])
    own_copy = remote(y_hbm, yfull.at[:, my_rows, :], f_send.at[0, 0], f_recv.at[0, 0], {"tensor": partner})
    own_copy.start()
    partner_rows = pl.ds(pl.multiple_of(partner * own, own), own)
    own_in = remote(y_hbm, yfull.at[:, partner_rows, :], f_send.at[0, 0], f_recv.at[0, 0], {"tensor": partner})

    loads[0].wait()
    loads[1].wait()
    r_parts = [split(r_ref[layer]) for layer in range(layers)]
    tiles = x_ref.shape[1] // own
    for tile in range(tiles):
        outs = []
        for layer in range(layers):
            block = x_ref[layer, tile * own : (tile + 1) * own, :]
            high, low = r_parts[layer]
            outs.append(dot(block, high, ((1,), (1,))) + dot(block, low, ((1,), (1,))))
        pt[tile] = jnp.concatenate(outs, axis=1).astype(pt.dtype)

    p_out = []
    for k in range(1, n_t):
        there = lax.rem(t + k, n_t)
        copy = remote(pt.at[there], pt_in.at[k - 1], p_send.at[k - 1], p_recv.at[k - 1], {"tensor": there})
        copy.start()
        p_out.append(copy)
    send_chunks(PLAN[1])

    loads[3].wait()
    loads[2].wait()
    own_y = pltpu.make_async_copy(y_ref, yfull.at[:, my_rows, :], yl_sem)
    own_y.start()
    block_rows = width // 6

    def left_of_error(i, carry):
        at = pl.ds(pl.multiple_of(i * block_rows, block_rows), block_rows)
        outs = []
        for layer in range(layers):
            block = e_ref[layer, at, :]
            high, low = r_parts[layer]
            outs.append(dot(block, high, ((1,), (1,))) + dot(block, low, ((1,), (1,))))
        lt[at, :] = jnp.concatenate(outs, axis=1)
        return carry

    lax.fori_loop(0, 6, left_of_error, 0)
    for copy in p_out:
        copy.wait()
    total = pt[t].astype(F32)
    for k in range(n_t - 1):
        total = total + pt_in[k].astype(F32)
    p_parts = [split(total[:, layer * rank : (layer + 1) * rank]) for layer in range(layers)]

    def left_of_tokens(i, carry):
        at = pl.ds(pl.multiple_of(i * block_rows, block_rows), block_rows)
        outs = []
        for layer in range(layers):
            block = y_ref[layer, :, at]
            high, low = p_parts[layer]
            outs.append(dot(block, high, ((0,), (0,))) + dot(block, low, ((0,), (0,))))
        lt[at, :] += jnp.concatenate(outs, axis=1)
        return carry

    lax.fori_loop(0, 6, left_of_tokens, 0)

    mine = pl.multiple_of(core * half, half)
    other = pl.multiple_of((1 - core) * half, half)
    core_copy = remote(lt.at[pl.ds(other, half), :], lt_core, c_send, c_recv, {"tensor": partner})
    core_copy.start()
    core_copy.wait()

    def add_core(j, carry):
        at = pl.ds(pl.multiple_of(mine + j * piece, piece), piece)
        value = lt[at, :] + lt_core[pl.ds(pl.multiple_of(j * piece, piece), piece), :]
        lt_send[j] = value.astype(lt_send.dtype)
        return carry

    lax.fori_loop(0, n_d, add_core, 0)
    d_out = []
    for k in range(1, n_d):
        there = lax.rem(d + k, n_d)
        copy = remote(lt_send.at[there], lt_in.at[k - 1], d_send.at[k - 1], d_recv.at[k - 1], {"dp": there})
        copy.start()
        d_out.append(copy)
    send_chunks(PLAN[2])
    pass_chunks(PLAN[0])
    for copy in d_out:
        copy.wait()
    total = lt_send[d].astype(F32)
    for k in range(n_d - 1):
        total = total + lt_in[k].astype(F32)
    lt_sum[...] = total.astype(lt_sum.dtype)
    total = lt_sum[...].astype(F32)
    s_out = []
    for m in range(1, n_y):
        there = lax.rem(t + 2 * m, n_t)
        copy = remote(lt_sum, lt_y.at[m - 1], s_send.at[m - 1], s_recv.at[m - 1], {"tensor": there})
        copy.start()
        s_out.append(copy)
    for copy in s_out:
        copy.wait()
    send_chunks(PLAN[3])
    for m in range(n_y - 1):
        total = total + lt_y[m].astype(F32)

    def slot(side, index):
        return ltf.at[pl.ds(pl.multiple_of(side * half + index * piece, piece), piece), :]

    ltf[pl.ds(pl.multiple_of(mine + d * piece, piece), piece), :] = total.astype(ltf.dtype)
    g_out = []
    for k in range(1, n_d):
        there = lax.rem(d + k, n_d)
        copy = remote(slot(core, d), slot(core, d), g_send.at[k - 1], g_recv.at[k - 1], {"dp": there})
        copy.start()
        g_out.append(copy)
    h_out = []
    for k in range(n_d):
        source = lax.rem(d + n_d - k, n_d)
        if k > 0:
            remote(slot(core, source), slot(core, source), g_send.at[k - 1], g_recv.at[k - 1], {"dp": source}).wait_recv()
        copy = remote(slot(core, source), slot(core, source), h_send.at[k], h_recv.at[k], {"tensor": partner})
        copy.start()
        h_out.append(copy)
    send_chunks(PLAN[4])
    pass_chunks(sum(PLAN[:3]))
    for k in range(n_d):
        source = lax.rem(d + n_d - k, n_d)
        remote(
            slot(1 - core, source), slot(1 - core, source), h_send.at[k], h_recv.at[k], {"tensor": partner}
        ).wait_recv()
    for copy in g_out + h_out:
        copy.wait_send()

    gram = jnp.zeros((layers * rank, layers * rank), F32)
    for i in range(6):
        block = ltf[i * block_rows : (i + 1) * block_rows, :].astype(F32)
        gram = gram + lax.dot_general(
            block, block, (((0,), (0,)), ((), ())), precision=HIGHEST, preferred_element_type=F32
        )
    grams = [gram[k * rank : (k + 1) * rank, k * rank : (k + 1) * rank] for k in range(layers)]
    inverses = inverse_factors(grams)
    zero = jnp.zeros((rank, rank), F32)
    spread = jnp.concatenate(
        [
            jnp.concatenate([inverses[i] if i == j else zero for j in range(layers)], axis=1)
            for i in range(layers)
        ],
        axis=0,
    )

    q = [jnp.zeros((own, 2 * rank), F32) for _ in range(layers)]
    right = [jnp.zeros((2 * rank, feats), F32) for _ in range(layers)]
    for i in range(6):
        at = slice(i * block_rows, (i + 1) * block_rows)
        basis = lax.dot_general(
            ltf[at, :].astype(F32), spread, (((1,), (1,)), ((), ())), precision=HIGHEST, preferred_element_type=F32
        )
        ot_ref[at, :] = basis
        for layer in range(layers):
            both = jnp.concatenate(split(basis[:, layer * rank : (layer + 1) * rank]), axis=1)
            q[layer] = q[layer] + dot(y_ref[layer, :, at], both, ((1,), (0,)))
    q_all[t] = jnp.concatenate([part[:, :rank] + part[:, rank:] for part in q], axis=1).astype(q_all.dtype)
    q_out = []
    for k in range(1, n_t):
        copy = remote(
            q_all.at[t], q_all.at[t], q_send.at[k - 1], q_recv.at[k - 1], {"tensor": lax.rem(t + k, n_t)}
        )
        copy.start()
        q_out.append(copy)
    send_chunks(PLAN[5])
    for i in range(6):
        at = slice(i * block_rows, (i + 1) * block_rows)
        for layer in range(layers):
            both = jnp.concatenate(split(ot_ref[at, layer * rank : (layer + 1) * rank]), axis=1)
            right[layer] = right[layer] + dot(both, e_ref[layer, at, :], ((0,), (0,)))
    for k in range(1, n_t):
        source = lax.rem(t + n_t - k, n_t)
        remote(
            q_all.at[source], q_all.at[source], q_send.at[k - 1], q_recv.at[k - 1], {"tensor": source}
        ).wait_recv()
    right = [part[:rank] + part[rank:] for part in right]
    for tile in range(tiles):
        value = q_all[tile]
        for layer in range(layers):
            part = value[:, layer * rank : (layer + 1) * rank]
            right[layer] = right[layer] + dot(part, x_ref[layer, tile * own : (tile + 1) * own, :], ((0,), (0,)))
    right_rows = jnp.concatenate(right, axis=0)
    share = layers * rank // n_d
    for j in range(n_d):
        r_send[j] = right_rows[j * share : (j + 1) * share, :].astype(BF16)
    a_out = []
    for k in range(1, n_d):
        there = lax.rem(d + k, n_d)
        copy = remote(r_send.at[there], r_in.at[k - 1], a_send.at[k - 1], a_recv.at[k - 1], {"dp": there})
        copy.start()
        a_out.append(copy)
    pass_chunks(10)
    for copy in a_out:
        copy.wait()
    total = r_send[d].astype(F32)
    for k in range(n_d - 1):
        total = total + r_in[k].astype(F32)
    r_all[d] = total.astype(BF16)
    b_out = []
    for k in range(1, n_d):
        copy = remote(r_all.at[d], r_all.at[d], b_send.at[k - 1], b_recv.at[k - 1], {"dp": lax.rem(d + k, n_d)})
        copy.start()
        b_out.append(copy)
    pass_chunks(len(chunks))
    for k in range(1, n_d):
        source = lax.rem(d + n_d - k, n_d)
        remote(r_all.at[source], r_all.at[source], b_send.at[k - 1], b_recv.at[k - 1], {"dp": source}).wait_recv()
    right_ref[...] = r_all[...]
    own_rows = width // n_d
    own_ref[...] = ot_ref[pl.ds(pl.multiple_of(d * own_rows, own_rows), own_rows), :]
    own_in.wait_recv()
    own_copy.wait_send()
    own_y.wait()
    for copy in q_out + b_out:
        copy.wait_send()
    for i in range(len(chunks)):
        for m in range(1, n_y):
            chunk_copy(i, m).wait_send()
            forward_copy(i, m).wait_send()
            forward_in(i, m).wait_recv()


def error_kernel(n_d, y_ref, x_ref, e_ref, o_ref, r_ref, own_ref, err_ref, sum_ref):
    layer = pl.program_id(0)
    wide = r_ref.shape[0]
    rank = wide // pl.num_programs(0)
    of_layer = lax.broadcasted_iota(jnp.int32, (1, wide), 1) // rank == layer

    def low_rank(basis):
        both = jnp.concatenate(split(jnp.where(of_layer, basis, 0.0)), axis=1)
        return dot(both, jnp.concatenate([r_ref[...], r_ref[...]], axis=0), ((1,), (0,)))

    moment = dot(y_ref[0], x_ref[0], ((0,), (0,))) + e_ref[0].astype(F32)
    err_ref[0] = (moment - low_rank(o_ref[...]) * (1.0 / n_d)).astype(err_ref.dtype)

    @pl.when(pl.program_id(1) == 0)
    def _():
        sum_ref[0] = low_rank(own_ref[...]).astype(sum_ref.dtype)


def solution(mesh):
    n_d, n_t = mesh.shape["dp"], mesh.shape["tensor"]

    def body(context, out_grad, error_in, right_init):
        layers, tokens, feats = context.shape
        own, width = out_grad.shape[1:]
        rank = right_init.shape[1]
        wide = layers * rank
        half = width // 2
        piece = half // n_d
        share = wide // n_d
        n_y = n_t // 2
        n_c = layers * CHUNKS
        rows = width // n_d
        dma = pltpu.SemaphoreType.DMA
        any_spec = pl.BlockSpec(memory_space=pl.ANY)
        vmem_spec = pl.BlockSpec(memory_space=pltpu.VMEM)
        pairs = lambda *shape: [dma(shape), dma(shape)]
        yfull, ortho, own_basis, right = pl.pallas_call(
            functools.partial(comm_kernel, n_d, n_t),
            name="low_rank_chain",
            out_shape=(
                jax.ShapeDtypeStruct((layers, tokens, width), BF16),
                jax.ShapeDtypeStruct((width, wide), F32),
                jax.ShapeDtypeStruct((rows, wide), F32),
                jax.ShapeDtypeStruct((n_d, share, feats), BF16),
            ),
            in_specs=[any_spec] * 4,
            out_specs=(any_spec, vmem_spec, vmem_spec, vmem_spec),
            scratch_shapes=[
                pltpu.VMEM((layers, tokens, feats), BF16),
                pltpu.VMEM((layers, own, width), BF16),
                pltpu.VMEM((layers, width, feats), BF16),
                pltpu.VMEM((layers, rank, feats), F32),
                pltpu.VMEM((n_t, own, wide), WIRE),
                pltpu.VMEM((n_t - 1, own, wide), WIRE),
                pltpu.VMEM((n_t, own, wide), WIRE),
                pltpu.VMEM((width, wide), F32),
                pltpu.VMEM((half, wide), F32),
                pltpu.VMEM((n_d, piece, wide), WIRE),
                pltpu.VMEM((n_d - 1, piece, wide), WIRE),
                pltpu.VMEM((max(n_y - 1, 1), piece, wide), WIRE),
                pltpu.VMEM((piece, wide), WIRE),
                pltpu.VMEM((width, wide), WIRE),
                pltpu.VMEM((n_d, share, feats), BF16),
                pltpu.VMEM((n_d - 1, share, feats), BF16),
                pltpu.VMEM((n_d, share, feats), BF16),
                dma((4,)),
                dma,
            ]
            + pairs(max(n_y - 1, 1), n_c)
            + pairs(n_y, n_c)
            + pairs(n_t - 1)
            + [dma, dma]
            + pairs(n_d - 1)
            + pairs(max(n_y - 1, 1))
            + pairs(n_d - 1)
            + pairs(n_d)
            + pairs(n_t - 1)
            + pairs(n_d - 1)
            + pairs(n_d - 1),
            compiler_params=pltpu.CompilerParams(
                collective_id=0, has_side_effects=True, vmem_limit_bytes=60 * 1024 * 1024
            ),
        )(context, out_grad, error_in, right_init)
        right = right.reshape(wide, feats)
        tile = width // 3
        new_error, summed = pl.pallas_call(
            functools.partial(error_kernel, n_d),
            name="new_error",
            grid=(layers, width // tile),
            out_shape=(
                jax.ShapeDtypeStruct((layers, width, feats), BF16),
                jax.ShapeDtypeStruct((layers, rows, feats), BF16),
            ),
            in_specs=[
                pl.BlockSpec((1, tokens, tile), lambda i, j: (i, 0, j)),
                pl.BlockSpec((1, tokens, feats), lambda i, j: (i, 0, 0)),
                pl.BlockSpec((1, tile, feats), lambda i, j: (i, j, 0)),
                pl.BlockSpec((tile, wide), lambda i, j: (j, 0)),
                pl.BlockSpec((wide, feats), lambda i, j: (0, 0)),
                pl.BlockSpec((rows, wide), lambda i, j: (0, 0)),
            ],
            out_specs=(
                pl.BlockSpec((1, tile, feats), lambda i, j: (i, j, 0)),
                pl.BlockSpec((1, rows, feats), lambda i, j: (i, 0, 0)),
            ),
            compiler_params=pltpu.CompilerParams(
                dimension_semantics=("arbitrary", "arbitrary"), vmem_limit_bytes=60 * 1024 * 1024
            ),
        )(yfull, context, error_in, ortho, right, own_basis)
        return summed, new_error

    return jax.shard_map(
        body,
        mesh=mesh,
        in_specs=(
            P(None, "dp", "tensor"),
            P(None, ("dp", "tensor"), None),
            P(None, "dp", "tensor"),
            P(None, None, "tensor"),
        ),
        out_specs=(P(None, "dp", "tensor"), P(None, "dp", "tensor")),
        check_vma=False,
    )
```
